256 devices in a mesh: seq: 64 (over x, z, core), head: 4 (over y).
Axes of the slice: x: 4, y: 4, z: 8, core: 2. Of those that a mesh axis runs over, the one named last changes fastest.
Arguments:
- queries: bfloat16 [16384, 64, 128], P(('seq', 'head')), may hold values from -64 to 64
- key_vectors: bfloat16 [16384, 64, 128], P(('seq', 'head')), may hold values from -5 to 5
- value_vectors: bfloat16 [16384, 64, 128], P(('seq', 'head')), may hold values from -6 to 6
- key_blocks: int32 [128, 12], P('seq'), may hold values from -1 to 125, as said below
Outputs:
- attended: bfloat16 [16384, 64, 128], P(('seq', 'head'))
The draws below stay inside these ranges and needn't reach their ends.
Inputs may be any that keep to these rules, and one draw needn't show every extreme that they name: `key_blocks`: entries 2j and 2j+1 of row b are -1 or distinct blocks c with c // 2 == b // 2 - 2**j, never b - 1.
All inputs are finite; a program needn't handle non-finite values.
Results may differ from the reference program's by a relative error of at most 0.004.
Values may be sent and summed in bfloat16 or wider, within the bound.
A program may use at most 192 MiB of HBM per device.

```python
import math
import jax
import jax.numpy as jnp
from jax import lax

HEADS = 64
HEAD_DIM = 128
BLOCK = 128
LEVELS = 6
BLK_DEV = 2
TOKENS = 16384
NB = 128


def pair_fields(key):
    base = jax.random.fold_in(key, 4242)
    key_query, key_other = jax.random.split(base)
    extent = (TOKENS, HEADS, HEAD_DIM)
    query_field = 2.5 * jnp.clip(jax.random.normal(key_query, extent, jnp.float32), -5.0, 5.0)
    key_field = jnp.clip(jax.random.normal(key_other, extent, jnp.float32), -5.0, 5.0)
    return (query_field, key_field)


def draw_queries(key, part):
    return pair_fields(key)[0].astype(jnp.bfloat16)


def draw_key_vectors(key, part):
    return pair_fields(key)[1].astype(jnp.bfloat16)


def draw_key_blocks(key, part):
    base = jax.random.fold_in(key, 777)
    random_bits = jax.random.randint(base, (NB, LEVELS, 4), 0, 1048576)
    block_index = jnp.arange(NB, dtype=jnp.int32)
    device = block_index // BLK_DEV
    within = block_index % BLK_DEV
    section_ids = jnp.arange(LEVELS, dtype=jnp.int32)
    distance = jnp.left_shift(jnp.int32(1), section_ids)
    partner = device[:, None] - distance[None, :]
    excluded = ((section_ids[None, :] == 0) & (within[:, None] == 0)).astype(jnp.int32)
    available = BLK_DEV - excluded
    first_pick = random_bits[:, :, 0] % available
    second_pick = (first_pick + 1 + random_bits[:, :, 1] % jnp.maximum(available - 1, 1)) % available
    first_here = random_bits[:, :, 2] % 4 != 0
    second_here = (random_bits[:, :, 3] % 2 == 0) & (available >= 2)
    reachable = partner >= 0
    first_entry = jnp.where(reachable & first_here, partner * BLK_DEV + first_pick, -1)
    second_entry = jnp.where(reachable & second_here, partner * BLK_DEV + second_pick, -1)
    table = jnp.stack([first_entry, second_entry], axis=2).reshape(NB, 2 * LEVELS).astype(jnp.int32)
    forced = jnp.int32(NB - BLK_DEV - 1)
    table = table.at[NB - 1, 0].set(forced)
    other = table[NB - 1, 1]
    return table.at[NB - 1, 1].set(jnp.where(other == forced, jnp.int32(-1), other))


def level_of(stream_key, shape, shards, low, high):
    level, own = 1.0, jax.random.fold_in(stream_key, 6)
    for dim, parts in shards:
        heights = jnp.exp(jax.random.uniform(jax.random.fold_in(own, dim), (parts,), jnp.float32, low / len(shards), high / len(shards)))
        level = level * jnp.repeat(heights, shape[dim] // parts).reshape([-1 if axis == dim else 1 for axis in range(len(shape))])
    return level


def scatter_about(rng, dims, width, bound, shards=(), kind=jnp.bfloat16):
    loudness = level_of(rng, dims, shards, -0.22, 0.18) if shards else 1.0
    entries = jax.random.normal(rng, dims, jnp.float32) * width * loudness
    return jnp.minimum(jnp.maximum(entries, -bound), bound).astype(kind)


def setup_inputs(seed: int = 0) -> dict:
    streams_of = jax.random.split(jax.random.key(seed), 5)
    return {
        "queries": draw_queries(jax.random.fold_in(streams_of[4], 71), 0),
        "key_vectors": draw_key_vectors(jax.random.fold_in(streams_of[4], 71), 0),
        "value_vectors": scatter_about(streams_of[2], (TOKENS, HEADS, HEAD_DIM), 1.0, 6.0, ((0, 256),)),
        "key_blocks": draw_key_blocks(jax.random.fold_in(streams_of[4], 71), 0),
    }


def reference(queries, key_vectors, value_vectors, key_blocks):
    block_total = queries.shape[0] // BLOCK
    head_count = queries.shape[1]
    head_width = queries.shape[2]
    query_tiles = queries.reshape(block_total, BLOCK, head_count, head_width)
    key_tiles = key_vectors.reshape(block_total, BLOCK, head_count, head_width)
    value_tiles = value_vectors.reshape(block_total, BLOCK, head_count, head_width)
    inverse_root = 1.0 / math.sqrt(head_width)
    causal = jnp.arange(BLOCK)[:, None] >= jnp.arange(BLOCK)[None, :]
    slot_count = key_blocks.shape[1] + 2
    first_slot = jnp.arange(slot_count) == 0

    def per_block(index):
        block_ids = jnp.concatenate([jnp.stack([index, index - 1]).astype(jnp.int32), key_blocks[index].astype(jnp.int32)])
        present = block_ids >= 0
        safe_ids = jnp.maximum(block_ids, 0)
        near_keys = key_tiles[safe_ids].astype(jnp.float32)
        near_values = value_tiles[safe_ids].astype(jnp.float32)
        query_block = query_tiles[index].astype(jnp.float32)
        scores = jnp.einsum('qhd,skhd->hqsk', query_block, near_keys) * inverse_root
        allowed = present[None, None, :, None] & (jnp.logical_not(first_slot)[None, None, :, None] | causal[None, :, None, :])
        scores = jnp.where(allowed, scores, jnp.float32(-1e+30))
        peak = lax.optimization_barrier(jnp.max(scores, axis=(2, 3), keepdims=True))
        weights = jnp.exp(scores - peak)
        norm_total = lax.optimization_barrier(jnp.sum(weights, axis=(2, 3)))
        rounded = lax.optimization_barrier(weights.astype(jnp.bfloat16)).astype(jnp.float32)
        summed = jnp.einsum('hqsk,skhd->qhd', rounded, near_values)
        return (summed / jnp.transpose(norm_total)[:, :, None]).astype(jnp.bfloat16)
    attended = lax.map(per_block, jnp.arange(block_total, dtype=jnp.int32))
    return attended.reshape(queries.shape)
```

```python
import math

import jax
import jax.numpy as jnp
from jax import lax
from jax.experimental import pallas as pl
from jax.experimental.pallas import tpu as pltpu
from jax.sharding import PartitionSpec as P

BLOCK = 128
LEVELS = 6
XS, ZS, CS, YS = 4, 8, 2, 4
PEERS = ZS * CS * YS
PAIRS = ZS * CS
PIECE = 64
NEG = -1e30
MESH = pl.DeviceIdType.MESH


def kernel(kb_ref, src_ref, out_ref, kv, qs, bias, own_bias, outs, scores, *sems):
    kv_send, kv_recv, q_send, q_recv, b_send, b_recv, x1_send, x1_recv, x2_send, x2_recv, o_send, o_recv = sems
    seq = lax.axis_index("seq")
    y = lax.axis_index("head")
    x = seq // (ZS * CS)
    pair = seq % PAIRS
    z = pair // CS
    core = pair % CS
    my_head = y * PAIRS + pair
    my_slot = pair * YS + y

    def device_of(x_, pair_, y_):
        return (x_ * PAIRS + pair_, y_)

    def offset(i):
        return i % ZS, (i // ZS) % CS, i // (ZS * CS)

    def toward(i):
        dz, dc, dy = offset(i)
        return ((z + dz) % ZS) * CS + (core + dc) % CS, (y + dy) % YS

    def behind(i):
        dz, dc, dy = offset(i)
        return ((z + ZS - dz) % ZS) * CS + (core + CS - dc) % CS, (y + YS - dy) % YS

    barrier = pltpu.get_barrier_semaphore()

    def greet(i, carry):
        pair_, y_ = toward(i)
        pl.semaphore_signal(barrier, inc=1, device_id=device_of(x, pair_, y_), device_id_type=MESH)
        return carry

    lax.fori_loop(1, PEERS, greet, 0)
    for step in (1, 2):
        @pl.when(x + step < XS)
        def _():
            pl.semaphore_signal(barrier, inc=1, device_id=device_of(x + step, pair, y), device_id_type=MESH)

        @pl.when(x >= step)
        def _():
            pl.semaphore_signal(barrier, inc=1, device_id=device_of(x - step, pair, y), device_id_type=MESH)

    for block in range(2):
        for level in range(LEVELS):
            for key in range(2):
                key_id = 2 * (seq - 2**level) + key
                hit = (kb_ref[block, 0] == key_id)
                for entry in range(1, 2 * LEVELS):
                    hit = hit | (kb_ref[block, entry] == key_id)
                hit = hit | (key_id == 2 * seq + block - 1)
                value = jnp.where(hit & (key_id >= 0), jnp.float32(0.0), jnp.float32(NEG))
                own_bias[block * 8 + level : block * 8 + level + 1, key * BLOCK : (key + 1) * BLOCK] = jnp.full(
                    (1, BLOCK), value, jnp.float32
                )

    @pl.when(x == 0)
    def _():
        kv[PEERS : 2 * PEERS] = jnp.zeros((PEERS, 2 * PIECE, 128), kv.dtype)

    @pl.when(x <= 1)
    def _():
        kv[0:PEERS] = jnp.zeros((PEERS, 2 * PIECE, 128), kv.dtype)

    near = 2 * PEERS

    own_kv = pltpu.make_async_copy(src_ref.at[my_head, pl.ds(0, 2 * PIECE)], kv.at[near + my_slot], kv_recv.at[0])
    own_q = pltpu.make_async_copy(src_ref.at[my_head, pl.ds(2 * PIECE, PIECE)], qs.at[my_slot], q_recv.at[0])
    own_kv.start()
    own_q.start()
    both = (x + 1 < XS).astype(jnp.int32) + (x + 2 < XS).astype(jnp.int32) + (x >= 1).astype(jnp.int32) + (x >= 2).astype(jnp.int32)
    pl.semaphore_wait(barrier, PEERS - 1 + both)

    def send_kv(i, carry):
        pair_, y_ = toward(i)
        pltpu.make_async_remote_copy(
            src_ref.at[y_ * PAIRS + pair_, pl.ds(0, 2 * PIECE)],
            kv.at[near + my_slot],
            kv_send.at[0],
            kv_recv.at[i],
            device_id=device_of(x, pair_, y_),
            device_id_type=MESH,
        ).start()
        return carry

    def send_q(i, carry):
        pair_, y_ = toward(i)
        pltpu.make_async_remote_copy(
            src_ref.at[y_ * PAIRS + pair_, pl.ds(2 * PIECE, PIECE)],
            qs.at[my_slot],
            q_send.at[0],
            q_recv.at[0],
            device_id=device_of(x, pair_, y_),
            device_id_type=MESH,
        ).start()
        return carry

    def send_bias(i, carry):
        pair_, y_ = toward(i)
        pltpu.make_async_remote_copy(
            own_bias, bias.at[pair], b_send.at[0], b_recv.at[0], device_id=device_of(x, pair_, y_), device_id_type=MESH
        ).start()
        return carry

    lax.fori_loop(1, PEERS, send_kv, 0)
    lax.fori_loop(1, PEERS, send_q, 0)
    own_b = pltpu.make_async_copy(own_bias, bias.at[pair], b_recv.at[0])
    own_b.start()
    lax.fori_loop(1, PAIRS, send_bias, 0)

    def forward(i, carry):
        pair_, y_ = behind(i)
        slot = pair_ * YS + y_
        here = kv.at[near + slot]
        pltpu.make_async_copy(here, here, kv_recv.at[i]).wait()
        for step, send, recv in ((1, x1_send, x1_recv), (2, x2_send, x2_recv)):
            @pl.when(x + step < XS)
            def _():
                pltpu.make_async_remote_copy(
                    here,
                    kv.at[near - step * PEERS + slot],
                    send.at[0],
                    recv.at[0],
                    device_id=device_of(x + step, pair, y),
                    device_id_type=MESH,
                ).start()
        return carry

    lax.fori_loop(0, PEERS, forward, 0)
    for step, recv in ((1, x1_recv), (2, x2_recv)):
        @pl.when(x >= step)
        def _():
            whole = kv.at[pl.ds(near - step * PEERS, PEERS)]
            pltpu.make_async_copy(whole, whole, recv.at[0]).wait()

    pltpu.make_async_copy(bias, bias, b_recv.at[0]).wait()
    pltpu.make_async_copy(qs, qs, q_recv.at[0]).wait()

    scale = math.log2(math.e) / math.sqrt(128.0)

    def half(p, d, part):
        return kv[pl.ds(YS * (2 * PAIRS + p - d), YS), part * PIECE : (part + 1) * PIECE, :].reshape(2 * BLOCK, 128)

    def attend(p):
        q = qs[pl.ds(YS * p, YS)].reshape(2 * BLOCK, 128)
        peak = None
        for level in range(LEVELS + 1):
            d = 0 if level == LEVELS else 2**level
            s = lax.dot_general(q, half(p, d, 0), (((1,), (1,)), ((), ())), preferred_element_type=jnp.float32)
            if d == 0:
                row = lax.broadcasted_iota(jnp.int32, (2 * BLOCK, 2 * BLOCK), 0)
                col = lax.broadcasted_iota(jnp.int32, (2 * BLOCK, 2 * BLOCK), 1)
                s = jnp.where(col <= row, s, NEG)
                scores[level] = s
            else:
                s0 = s[0:BLOCK] + bias[p, level : level + 1, :]
                s1 = s[BLOCK:] + bias[p, 8 + level : 9 + level, :]
                s = jnp.concatenate([s0, s1], axis=0)
                scores[level] = s
            top = jnp.maximum(s[:, 0:BLOCK], s[:, BLOCK:])
            peak = top if peak is None else jnp.maximum(peak, top)
        peak = jnp.max(peak, axis=1, keepdims=True)
        total = None
        acc = None
        for level in range(LEVELS + 1):
            d = 0 if level == LEVELS else 2**level
            w = jnp.exp2((scores[level] - peak) * scale)
            part = w[:, 0:BLOCK] + w[:, BLOCK:]
            total = part if total is None else total + part
            o = jnp.dot(w.astype(jnp.bfloat16), half(p, d, 1), preferred_element_type=jnp.float32)
            acc = o if acc is None else acc + o
        norm = jnp.sum(total, axis=1, keepdims=True)
        outs[pl.ds(YS * p, YS)] = (acc / norm).astype(jnp.bfloat16).reshape(YS, PIECE, 128)

    def give_back(p):
        for y_ in range(YS):
            here = outs.at[YS * p + y_]
            there = out_ref.at[my_head]
            mine = (p == pair) & (y == y_)

            @pl.when(mine)
            def _():
                pltpu.make_async_copy(here, there, o_recv.at[0]).start()

            @pl.when(jnp.logical_not(mine))
            def _():
                pltpu.make_async_remote_copy(
                    here, there, o_send.at[0], o_recv.at[0], device_id=device_of(x, p, y_), device_id_type=MESH
                ).start()

    def step(k, carry):
        attend((pair + k) % PAIRS)

        @pl.when(k >= 1)
        def _():
            give_back((pair + k + PAIRS - 1) % PAIRS)

        return carry

    lax.fori_loop(0, PAIRS, step, 0)
    give_back((pair + PAIRS - 1) % PAIRS)

    most = kv.at[pl.ds(near, PEERS - 1)]
    pltpu.make_async_copy(most, most, kv_send.at[0]).wait()
    most = qs.at[pl.ds(0, PEERS - 1)]
    pltpu.make_async_copy(most, most, q_send.at[0]).wait()
    most = bias.at[pl.ds(0, PAIRS - 1)]
    pltpu.make_async_copy(most, most, b_send.at[0]).wait()
    for step_, send in ((1, x1_send), (2, x2_send)):
        @pl.when(x + step_ < XS)
        def _():
            whole = kv.at[pl.ds(near, PEERS)]
            pltpu.make_async_copy(whole, whole, send.at[0]).wait()
    most = outs.at[pl.ds(0, PEERS - 1)]
    pltpu.make_async_copy(most, most, o_send.at[0]).wait()
    pltpu.make_async_copy(out_ref, out_ref, o_recv.at[0]).wait()


def local(queries, key_vectors, value_vectors, key_blocks):
    rows = jnp.concatenate([key_vectors, value_vectors, queries], axis=0)
    by_head = jnp.transpose(rows, (1, 0, 2))
    dma = pltpu.SemaphoreType.DMA
    result = pl.pallas_call(
        kernel,
        out_shape=jax.ShapeDtypeStruct((PEERS, PIECE, 128), jnp.bfloat16),
        in_specs=[pl.BlockSpec(memory_space=pltpu.SMEM), pl.BlockSpec(memory_space=pltpu.VMEM)],
        out_specs=pl.BlockSpec(memory_space=pltpu.VMEM),
        scratch_shapes=[
            pltpu.VMEM((3 * PEERS, 2 * PIECE, 128), jnp.bfloat16),
            pltpu.VMEM((PEERS, PIECE, 128), jnp.bfloat16),
            pltpu.VMEM((PAIRS, 16, 2 * BLOCK), jnp.float32),
            pltpu.VMEM((16, 2 * BLOCK), jnp.float32),
            pltpu.VMEM((PEERS, PIECE, 128), jnp.bfloat16),
            pltpu.VMEM((LEVELS + 1, 2 * BLOCK, 2 * BLOCK), jnp.float32),
            dma((1,)), dma((PEERS,)),
            dma((1,)), dma((1,)),
            dma((1,)), dma((1,)),
            dma((1,)), dma((1,)),
            dma((1,)), dma((1,)),
            dma((1,)), dma((1,)),
        ],
        compiler_params=pltpu.CompilerParams(collective_id=0, has_side_effects=True, vmem_limit_bytes=48 * 2**20),
    )(key_blocks, by_head)
    return jnp.transpose(result, (1, 0, 2))


def solution(mesh):
    return jax.shard_map(
        local,
        mesh=mesh,
        in_specs=(
            P(("seq", "head"), None, None),
            P(("seq", "head"), None, None),
            P(("seq", "head"), None, None),
            P("seq", None),
        ),
        out_specs=P(("seq", "head"), None, None),
        check_vma=False,
    )
```

```python
import math

import jax
import jax.numpy as jnp
from jax import lax
from jax.experimental import pallas as pl
from jax.experimental.pallas import tpu as pltpu
from jax.sharding import PartitionSpec as P

BLOCK = 128
LEVELS = 6
XS, ZS, CS, YS = 4, 8, 2, 4
PEERS = ZS * CS * YS
PAIRS = ZS * CS
PIECE = 64
NEG = -1e30
MESH = pl.DeviceIdType.MESH


RELAY = 3
AHEAD = PEERS // RELAY + 1
BACK = PEERS - AHEAD
LAG = 8


def kernel(kb_ref, src_ref, out_ref, kv, stage, qs, bias, own_bias, outs, scores, *sems):
    kv_send, kv_recv, q_send, q_recv, b_send, b_recv = sems[:6]
    up_send, upa_recv, upb_recv, down_send, down_recv, on_send, two_recv, o_send, o_recv = sems[6:]
    seq = lax.axis_index("seq")
    y = lax.axis_index("head")
    x = seq // (ZS * CS)
    pair = seq % PAIRS
    z = pair // CS
    core = pair % CS
    my_head = y * PAIRS + pair
    my_slot = pair * YS + y

    def device_of(x_, pair_, y_):
        return (x_ * PAIRS + pair_, y_)

    def offset(i):
        j = i // (CS * YS)
        return ((j + 1) // 2) * (2 * (j % 2) - 1) + ZS, (i // YS) % CS, i % YS

    def toward(i):
        dz, dc, dy = offset(i)
        return ((z + dz) % ZS) * CS + (core + dc) % CS, (y + dy) % YS

    def behind(i):
        dz, dc, dy = offset(i)
        return ((z + 2 * ZS - dz) % ZS) * CS + (core + CS - dc) % CS, (y + YS - dy) % YS

    barrier = pltpu.get_barrier_semaphore()

    def greet(i, carry):
        pair_, y_ = toward(i)
        pl.semaphore_signal(barrier, inc=1, device_id=device_of(x, pair_, y_), device_id_type=MESH)
        return carry

    lax.fori_loop(1, PEERS, greet, 0)
    x_up, x_down = (x + 1) % XS, (x + XS - 1) % XS
    for x_ in (x_up, x_down):
        pl.semaphore_signal(barrier, inc=1, device_id=device_of(x_, pair, y), device_id_type=MESH)

    for block in range(2):
        for level in range(LEVELS):
            for key in range(2):
                key_id = 2 * (seq - 2**level) + key
                hit = (kb_ref[block, 0] == key_id)
                for entry in range(1, 2 * LEVELS):
                    hit = hit | (kb_ref[block, entry] == key_id)
                hit = hit | (key_id == 2 * seq + block - 1)
                value = jnp.where(hit & (key_id >= 0), jnp.float32(0.0), jnp.float32(NEG))
                own_bias[block * 8 + level : block * 8 + level + 1, key * BLOCK : (key + 1) * BLOCK] = jnp.full(
                    (1, BLOCK), value, jnp.float32
                )

    @pl.when(x == 0)
    def _():
        kv[PEERS : 2 * PEERS] = jnp.zeros((PEERS, 2 * PIECE, 128), kv.dtype)

    @pl.when(x <= 1)
    def _():
        kv[0:PEERS] = jnp.zeros((PEERS, 2 * PIECE, 128), kv.dtype)

    near = 2 * PEERS

    own_kv = pltpu.make_async_copy(src_ref.at[my_head, pl.ds(0, 2 * PIECE)], kv.at[near + my_slot], kv_recv.at[0])
    own_q = pltpu.make_async_copy(src_ref.at[my_head, pl.ds(2 * PIECE, PIECE)], qs.at[my_slot], q_recv.at[pair])
    own_kv.start()
    own_q.start()
    pl.semaphore_wait(barrier, PEERS - 1 + 2)

    def send_kv(i, carry):
        pair_, y_ = toward(i)
        pltpu.make_async_remote_copy(
            src_ref.at[y_ * PAIRS + pair_, pl.ds(0, 2 * PIECE)],
            kv.at[near + my_slot],
            kv_send.at[0],
            kv_recv.at[i],
            device_id=device_of(x, pair_, y_),
            device_id_type=MESH,
        ).start()
        return carry

    def send_q(i, carry):
        pair_, y_ = toward(i)
        pltpu.make_async_remote_copy(
            src_ref.at[y_ * PAIRS + pair_, pl.ds(2 * PIECE, PIECE)],
            qs.at[my_slot],
            q_send.at[0],
            q_recv.at[pair],
            device_id=device_of(x, pair_, y_),
            device_id_type=MESH,
        ).start()
        return carry

    def send_bias(i, carry):
        pair_, y_ = toward(YS * i)
        pltpu.make_async_remote_copy(
            own_bias, bias.at[pair], b_send.at[0], b_recv.at[0], device_id=device_of(x, pair_, y_), device_id_type=MESH
        ).start()
        return carry

    lax.fori_loop(1, PEERS, send_kv, 0)
    lax.fori_loop(1, PEERS, send_q, 0)
    own_b = pltpu.make_async_copy(own_bias, bias.at[pair], b_recv.at[0])
    own_b.start()
    lax.fori_loop(1, PAIRS, send_bias, 0)

    def arrived(piece, recv):
        pltpu.make_async_copy(piece, piece, recv).wait()

    def piece_of(i):
        pair_, y_ = behind(i)
        return pair_ * YS + y_

    def pass_on(source, target, send, recv, x_):
        pltpu.make_async_remote_copy(
            source, target, send, recv, device_id=device_of(x_, pair, y), device_id_type=MESH
        ).start()

    def forward(i):
        slot = piece_of(i)
        here = kv.at[near + slot]
        arrived(here, kv_recv.at[i])
        ahead = i % RELAY == 0

        @pl.when((x < XS - 1) & ahead)
        def _():
            pass_on(here, kv.at[near - PEERS + slot], up_send.at[0], upa_recv.at[i // RELAY], x_up)

        @pl.when((x < XS - 1) & jnp.logical_not(ahead))
        def _():
            pass_on(here, kv.at[near - PEERS + slot], up_send.at[0], upb_recv.at[0], x_up)

        @pl.when((x < 2) & jnp.logical_not(ahead))
        def _():
            pass_on(here, stage.at[slot], down_send.at[0], down_recv.at[i], x_down)

    def relay(i):
        slot = piece_of(i)
        ahead = i % RELAY == 0

        @pl.when((x >= 1) & ahead)
        def _():
            here = kv.at[near - PEERS + slot]
            arrived(here, upa_recv.at[i // RELAY])

            @pl.when(x < XS - 1)
            def _():
                pass_on(here, kv.at[slot], on_send.at[0], two_recv.at[0], x_up)

        @pl.when(((x == 0) | (x == XS - 1)) & jnp.logical_not(ahead))
        def _():
            here = stage.at[slot]
            arrived(here, down_recv.at[i])
            pass_on(here, kv.at[slot], on_send.at[0], two_recv.at[0], x_down)

    def both_steps(i, carry):
        forward(i)

        @pl.when(i >= LAG)
        def _():
            relay(i - LAG)

        return carry

    lax.fori_loop(0, PEERS, both_steps, 0)

    def last_steps(i, carry):
        relay(i)
        return carry

    lax.fori_loop(PEERS - LAG, PEERS, last_steps, 0)

    @pl.when(x >= 1)
    def _():
        arrived(kv.at[pl.ds(near - PEERS, BACK)], upb_recv.at[0])

    @pl.when(x >= 2)
    def _():
        arrived(kv.at[pl.ds(0, PEERS)], two_recv.at[0])

    arrived(bias, b_recv.at[0])

    scale = math.log2(math.e) / math.sqrt(128.0)

    def half(p, d, part):
        return kv[pl.ds(YS * (2 * PAIRS + p - d), YS), part * PIECE : (part + 1) * PIECE, :].reshape(2 * BLOCK, 128)

    def attend(p):
        q = qs[pl.ds(YS * p, YS)].reshape(2 * BLOCK, 128)
        peak = None
        for level in range(LEVELS + 1):
            d = 0 if level == LEVELS else 2**level
            s = lax.dot_general(q, half(p, d, 0), (((1,), (1,)), ((), ())), preferred_element_type=jnp.float32)
            if d == 0:
                row = lax.broadcasted_iota(jnp.int32, (2 * BLOCK, 2 * BLOCK), 0)
                col = lax.broadcasted_iota(jnp.int32, (2 * BLOCK, 2 * BLOCK), 1)
                s = jnp.where(col <= row, s, NEG)
                scores[level] = s
            else:
                s0 = s[0:BLOCK] + bias[p, level : level + 1, :]
                s1 = s[BLOCK:] + bias[p, 8 + level : 9 + level, :]
                s = jnp.concatenate([s0, s1], axis=0)
                scores[level] = s
            top = jnp.maximum(s[:, 0:BLOCK], s[:, BLOCK:])
            peak = top if peak is None else jnp.maximum(peak, top)
        peak = jnp.max(peak, axis=1, keepdims=True)
        total = None
        acc = None
        for level in range(LEVELS + 1):
            d = 0 if level == LEVELS else 2**level
            w = jnp.exp2((scores[level] - peak) * scale)
            part = w[:, 0:BLOCK] + w[:, BLOCK:]
            total = part if total is None else total + part
            o = jnp.dot(w.astype(jnp.bfloat16), half(p, d, 1), preferred_element_type=jnp.float32)
            acc = o if acc is None else acc + o
        norm = jnp.sum(total, axis=1, keepdims=True)
        outs[pl.ds(YS * p, YS)] = (acc / norm).astype(jnp.bfloat16).reshape(YS, PIECE, 128)

    def give_back(p):
        for y_ in range(YS):
            here = outs.at[YS * p + y_]
            there = out_ref.at[my_head]
            mine = (p == pair) & (y == y_)

            @pl.when(mine)
            def _():
                pltpu.make_async_copy(here, there, o_recv.at[0]).start()

            @pl.when(jnp.logical_not(mine))
            def _():
                pltpu.make_async_remote_copy(
                    here, there, o_send.at[0], o_recv.at[0], device_id=device_of(x, p, y_), device_id_type=MESH
                ).start()

    def turn(k):
        return toward(YS * k)[0]

    def step(k, carry):
        p = turn(k)
        arrived(qs.at[pl.ds(YS * p, YS)], q_recv.at[p])
        attend(p)

        @pl.when(k >= 1)
        def _():
            give_back(turn(k - 1))

        return carry

    lax.fori_loop(0, PAIRS, step, 0)
    give_back(turn(PAIRS - 1))

    arrived(kv.at[pl.ds(near, PEERS - 1)], kv_send.at[0])
    arrived(qs.at[pl.ds(0, PEERS - 1)], q_send.at[0])
    arrived(bias.at[pl.ds(0, PAIRS - 1)], b_send.at[0])

    @pl.when(x < XS - 1)
    def _():
        arrived(kv.at[pl.ds(near, PEERS)], up_send.at[0])

    @pl.when(x < 2)
    def _():
        arrived(stage.at[pl.ds(0, BACK)], down_send.at[0])

    @pl.when((x >= 1) & (x < XS - 1))
    def _():
        arrived(kv.at[pl.ds(0, AHEAD)], on_send.at[0])

    @pl.when((x == 0) | (x == XS - 1))
    def _():
        arrived(kv.at[pl.ds(0, BACK)], on_send.at[0])

    arrived(outs.at[pl.ds(0, PEERS - 1)], o_send.at[0])
    arrived(out_ref, o_recv.at[0])


def local(queries, key_vectors, value_vectors, key_blocks):
    rows = jnp.concatenate([key_vectors, value_vectors, queries], axis=0)
    by_head = jnp.transpose(rows, (1, 0, 2))
    dma = pltpu.SemaphoreType.DMA
    result = pl.pallas_call(
        kernel,
        out_shape=jax.ShapeDtypeStruct((PEERS, PIECE, 128), jnp.bfloat16),
        in_specs=[pl.BlockSpec(memory_space=pltpu.SMEM), pl.BlockSpec(memory_space=pltpu.VMEM)],
        out_specs=pl.BlockSpec(memory_space=pltpu.VMEM),
        scratch_shapes=[
            pltpu.VMEM((3 * PEERS, 2 * PIECE, 128), jnp.bfloat16),
            pltpu.VMEM((PEERS, 2 * PIECE, 128), jnp.bfloat16),
            pltpu.VMEM((PEERS, PIECE, 128), jnp.bfloat16),
            pltpu.VMEM((PAIRS, 16, 2 * BLOCK), jnp.float32),
            pltpu.VMEM((16, 2 * BLOCK), jnp.float32),
            pltpu.VMEM((PEERS, PIECE, 128), jnp.bfloat16),
            pltpu.VMEM((LEVELS + 1, 2 * BLOCK, 2 * BLOCK), jnp.float32),
            dma((1,)), dma((PEERS,)),
            dma((1,)), dma((PAIRS,)),
            dma((1,)), dma((1,)),
            dma((1,)), dma((AHEAD,)), dma((1,)),
            dma((1,)), dma((PEERS,)),
            dma((1,)), dma((1,)),
            dma((1,)), dma((1,)),
        ],
        compiler_params=pltpu.CompilerParams(collective_id=0, has_side_effects=True, vmem_limit_bytes=48 * 2**20),
    )(key_blocks, by_head)
    return jnp.transpose(result, (1, 0, 2))


def solution(mesh):
    return jax.shard_map(
        local,
        mesh=mesh,
        in_specs=(
            P(("seq", "head"), None, None),
            P(("seq", "head"), None, None),
            P(("seq", "head"), None, None),
            P("seq", None),
        ),
        out_specs=P(("seq", "head"), None, None),
        check_vma=False,
    )
```

```python
import math

import jax
import jax.numpy as jnp
from jax import lax
from jax.experimental import pallas as pl
from jax.experimental.pallas import tpu as pltpu
from jax.sharding import PartitionSpec as P

BLOCK = 128
LEVELS = 6
XS, ZS, CS, YS = 4, 8, 2, 4
PEERS = ZS * CS * YS
PAIRS = ZS * CS
PIECE = 64
NEG = -1e30
MESH = pl.DeviceIdType.MESH


RELAY = 3
AHEAD = PEERS // RELAY + 1
BACK = PEERS - AHEAD
WINDOW = 32
LAG = 8


def kernel(kb_ref, src_ref, out_ref, kv, stage, qs, bias, own_bias, outs, scores, *sems):
    kv_send, kv_recv, q_send, q_recv, b_send, b_recv = sems[:6]
    up_send, upa_recv, upb_recv, down_send, down_recv, on_send, two_recv, o_send, o_recv = sems[6:]
    seq = lax.axis_index("seq")
    y = lax.axis_index("head")
    x = seq // (ZS * CS)
    pair = seq % PAIRS
    z = pair // CS
    core = pair % CS
    my_head = y * PAIRS + pair
    my_slot = pair * YS + y

    def device_of(x_, pair_, y_):
        return (x_ * PAIRS + pair_, y_)

    def offset(i):
        j = i // (CS * YS)
        return ((j + 1) // 2) * (2 * (j % 2) - 1) + ZS, (i // YS) % CS, i % YS

    def toward(i):
        dz, dc, dy = offset(i)
        return ((z + dz) % ZS) * CS + (core + dc) % CS, (y + dy) % YS

    def behind(i):
        dz, dc, dy = offset(i)
        return ((z + 2 * ZS - dz) % ZS) * CS + (core + CS - dc) % CS, (y + YS - dy) % YS

    barrier = pltpu.get_barrier_semaphore()

    def greet(i, carry):
        pair_, y_ = toward(i)
        pl.semaphore_signal(barrier, inc=1, device_id=device_of(x, pair_, y_), device_id_type=MESH)
        return carry

    lax.fori_loop(1, PEERS, greet, 0)
    x_up, x_down = (x + 1) % XS, (x + XS - 1) % XS
    for x_ in (x_up, x_down):
        pl.semaphore_signal(barrier, inc=1, device_id=device_of(x_, pair, y), device_id_type=MESH)

    for block in range(2):
        for level in range(LEVELS):
            for key in range(2):
                key_id = 2 * (seq - 2**level) + key
                hit = (kb_ref[block, 0] == key_id)
                for entry in range(1, 2 * LEVELS):
                    hit = hit | (kb_ref[block, entry] == key_id)
                hit = hit | (key_id == 2 * seq + block - 1)
                value = jnp.where(hit & (key_id >= 0), jnp.float32(0.0), jnp.float32(NEG))
                own_bias[block * 8 + level : block * 8 + level + 1, key * BLOCK : (key + 1) * BLOCK] = jnp.full(
                    (1, BLOCK), value, jnp.float32
                )

    @pl.when(x == 0)
    def _():
        kv[PEERS : 2 * PEERS] = jnp.zeros((PEERS, 2 * PIECE, 128), kv.dtype)

    @pl.when(x <= 1)
    def _():
        kv[0:PEERS] = jnp.zeros((PEERS, 2 * PIECE, 128), kv.dtype)

    near = 2 * PEERS

    own_kv = pltpu.make_async_copy(src_ref.at[my_head, pl.ds(0, 2 * PIECE)], kv.at[near + my_slot], kv_recv.at[0])
    own_q = pltpu.make_async_copy(src_ref.at[my_head, pl.ds(2 * PIECE, PIECE)], qs.at[my_slot], q_recv.at[pair])
    own_kv.start()
    own_q.start()
    pl.semaphore_wait(barrier, PEERS - 1 + 2)

    def send_kv(i, carry):
        pair_, y_ = toward(i)
        pltpu.make_async_remote_copy(
            src_ref.at[y_ * PAIRS + pair_, pl.ds(0, 2 * PIECE)],
            kv.at[near + my_slot],
            kv_send.at[0],
            kv_recv.at[i],
            device_id=device_of(x, pair_, y_),
            device_id_type=MESH,
        ).start()
        return carry

    def send_q(i, carry):
        pair_, y_ = toward(PEERS - i)
        pltpu.make_async_remote_copy(
            src_ref.at[y_ * PAIRS + pair_, pl.ds(2 * PIECE, PIECE)],
            qs.at[my_slot],
            q_send.at[0],
            q_recv.at[pair],
            device_id=device_of(x, pair_, y_),
            device_id_type=MESH,
        ).start()
        return carry

    def send_bias(i, carry):
        pair_, y_ = toward(YS * i)
        pltpu.make_async_remote_copy(
            own_bias, bias.at[pair], b_send.at[0], b_recv.at[0], device_id=device_of(x, pair_, y_), device_id_type=MESH
        ).start()
        return carry

    lax.fori_loop(1, WINDOW, send_kv, 0)
    own_b = pltpu.make_async_copy(own_bias, bias.at[pair], b_recv.at[0])
    own_b.start()
    lax.fori_loop(1, PAIRS, send_bias, 0)

    def arrived(piece, recv):
        pltpu.make_async_copy(piece, piece, recv).wait()

    def piece_of(i):
        pair_, y_ = behind(i)
        return pair_ * YS + y_

    def pass_on(source, target, send, recv, x_):
        pltpu.make_async_remote_copy(
            source, target, send, recv, device_id=device_of(x_, pair, y), device_id_type=MESH
        ).start()

    def forward(i):
        slot = piece_of(i)
        here = kv.at[near + slot]
        arrived(here, kv_recv.at[i])
        ahead = i % RELAY == 0

        @pl.when((x < XS - 1) & ahead)
        def _():
            pass_on(here, kv.at[near - PEERS + slot], up_send.at[0], upa_recv.at[i // RELAY], x_up)

        @pl.when((x < XS - 1) & jnp.logical_not(ahead))
        def _():
            pass_on(here, kv.at[near - PEERS + slot], up_send.at[0], upb_recv.at[0], x_up)

        @pl.when((x < 2) & jnp.logical_not(ahead))
        def _():
            pass_on(here, stage.at[slot], down_send.at[0], down_recv.at[i], x_down)

    def relay(i):
        slot = piece_of(i)
        ahead = i % RELAY == 0

        @pl.when((x >= 1) & ahead)
        def _():
            here = kv.at[near - PEERS + slot]
            arrived(here, upa_recv.at[i // RELAY])

            @pl.when(x < XS - 1)
            def _():
                pass_on(here, kv.at[slot], on_send.at[0], two_recv.at[0], x_up)

        @pl.when(((x == 0) | (x == XS - 1)) & jnp.logical_not(ahead))
        def _():
            here = stage.at[slot]
            arrived(here, down_recv.at[i])
            pass_on(here, kv.at[slot], on_send.at[0], two_recv.at[0], x_down)

    def both_steps(i, carry):
        forward(i)

        @pl.when(i + WINDOW < PEERS)
        def _():
            send_kv(i + WINDOW, 0)

        @pl.when(i + WINDOW >= PEERS)
        def _():
            first = 1 + 2 * (i + WINDOW - PEERS)
            lax.fori_loop(first, jnp.minimum(first + 2, PEERS), send_q, 0)

        @pl.when(i >= LAG)
        def _():
            relay(i - LAG)

        return carry

    lax.fori_loop(0, PEERS, both_steps, 0)

    def last_steps(i, carry):
        relay(i)
        return carry

    lax.fori_loop(PEERS - LAG, PEERS, last_steps, 0)

    @pl.when(x >= 1)
    def _():
        arrived(kv.at[pl.ds(near - PEERS, BACK)], upb_recv.at[0])

    @pl.when(x >= 2)
    def _():
        arrived(kv.at[pl.ds(0, PEERS)], two_recv.at[0])

    arrived(bias, b_recv.at[0])

    scale = math.log2(math.e) / math.sqrt(128.0)

    def half(p, d, part):
        return kv[pl.ds(YS * (2 * PAIRS + p - d), YS), part * PIECE : (part + 1) * PIECE, :].reshape(2 * BLOCK, 128)

    def attend(p):
        q = qs[pl.ds(YS * p, YS)].reshape(2 * BLOCK, 128)
        peak = None
        for level in range(LEVELS + 1):
            d = 0 if level == LEVELS else 2**level
            s = lax.dot_general(q, half(p, d, 0), (((1,), (1,)), ((), ())), preferred_element_type=jnp.float32)
            if d == 0:
                row = lax.broadcasted_iota(jnp.int32, (2 * BLOCK, 2 * BLOCK), 0)
                col = lax.broadcasted_iota(jnp.int32, (2 * BLOCK, 2 * BLOCK), 1)
                s = jnp.where(col <= row, s, NEG)
                scores[level] = s
            else:
                s0 = s[0:BLOCK] + bias[p, level : level + 1, :]
                s1 = s[BLOCK:] + bias[p, 8 + level : 9 + level, :]
                s = jnp.concatenate([s0, s1], axis=0)
                scores[level] = s
            top = jnp.maximum(s[:, 0:BLOCK], s[:, BLOCK:])
            peak = top if peak is None else jnp.maximum(peak, top)
        peak = jnp.max(peak, axis=1, keepdims=True)
        total = None
        acc = None
        for level in range(LEVELS + 1):
            d = 0 if level == LEVELS else 2**level
            w = jnp.exp2((scores[level] - peak) * scale)
            part = w[:, 0:BLOCK] + w[:, BLOCK:]
            total = part if total is None else total + part
            o = jnp.dot(w.astype(jnp.bfloat16), half(p, d, 1), preferred_element_type=jnp.float32)
            acc = o if acc is None else acc + o
        norm = jnp.sum(total, axis=1, keepdims=True)
        outs[pl.ds(YS * p, YS)] = (acc / norm).astype(jnp.bfloat16).reshape(YS, PIECE, 128)

    def give_back(p):
        for y_ in range(YS):
            here = outs.at[YS * p + y_]
            there = out_ref.at[my_head]
            mine = (p == pair) & (y == y_)

            @pl.when(mine)
            def _():
                pltpu.make_async_copy(here, there, o_recv.at[0]).start()

            @pl.when(jnp.logical_not(mine))
            def _():
                pltpu.make_async_remote_copy(
                    here, there, o_send.at[0], o_recv.at[0], device_id=device_of(x, p, y_), device_id_type=MESH
                ).start()

    def turn(k):
        return toward(YS * (PAIRS - 1 - k))[0]

    def step(k, carry):
        p = turn(k)
        arrived(qs.at[pl.ds(YS * p, YS)], q_recv.at[p])
        attend(p)

        @pl.when(k >= 1)
        def _():
            give_back(turn(k - 1))

        return carry

    lax.fori_loop(0, PAIRS, step, 0)
    give_back(turn(PAIRS - 1))

    arrived(kv.at[pl.ds(near, PEERS - 1)], kv_send.at[0])
    arrived(qs.at[pl.ds(0, PEERS - 1)], q_send.at[0])
    arrived(bias.at[pl.ds(0, PAIRS - 1)], b_send.at[0])

    @pl.when(x < XS - 1)
    def _():
        arrived(kv.at[pl.ds(near, PEERS)], up_send.at[0])

    @pl.when(x < 2)
    def _():
        arrived(stage.at[pl.ds(0, BACK)], down_send.at[0])

    @pl.when((x >= 1) & (x < XS - 1))
    def _():
        arrived(kv.at[pl.ds(0, AHEAD)], on_send.at[0])

    @pl.when((x == 0) | (x == XS - 1))
    def _():
        arrived(kv.at[pl.ds(0, BACK)], on_send.at[0])

    arrived(outs.at[pl.ds(0, PEERS - 1)], o_send.at[0])
    arrived(out_ref, o_recv.at[0])


def local(queries, key_vectors, value_vectors, key_blocks):
    rows = jnp.concatenate([key_vectors, value_vectors, queries], axis=0)
    by_head = jnp.transpose(rows, (1, 0, 2))
    dma = pltpu.SemaphoreType.DMA
    result = pl.pallas_call(
        kernel,
        out_shape=jax.ShapeDtypeStruct((PEERS, PIECE, 128), jnp.bfloat16),
        in_specs=[pl.BlockSpec(memory_space=pltpu.SMEM), pl.BlockSpec(memory_space=pltpu.VMEM)],
        out_specs=pl.BlockSpec(memory_space=pltpu.VMEM),
        scratch_shapes=[
            pltpu.VMEM((3 * PEERS, 2 * PIECE, 128), jnp.bfloat16),
            pltpu.VMEM((PEERS, 2 * PIECE, 128), jnp.bfloat16),
            pltpu.VMEM((PEERS, PIECE, 128), jnp.bfloat16),
            pltpu.VMEM((PAIRS, 16, 2 * BLOCK), jnp.float32),
            pltpu.VMEM((16, 2 * BLOCK), jnp.float32),
            pltpu.VMEM((PEERS, PIECE, 128), jnp.bfloat16),
            pltpu.VMEM((LEVELS + 1, 2 * BLOCK, 2 * BLOCK), jnp.float32),
            dma((1,)), dma((PEERS,)),
            dma((1,)), dma((PAIRS,)),
            dma((1,)), dma((1,)),
            dma((1,)), dma((AHEAD,)), dma((1,)),
            dma((1,)), dma((PEERS,)),
            dma((1,)), dma((1,)),
            dma((1,)), dma((1,)),
        ],
        compiler_params=pltpu.CompilerParams(collective_id=0, has_side_effects=True, vmem_limit_bytes=48 * 2**20),
    )(key_blocks, by_head)
    return jnp.transpose(result, (1, 0, 2))


def solution(mesh):
    return jax.shard_map(
        local,
        mesh=mesh,
        in_specs=(
            P(("seq", "head"), None, None),
            P(("seq", "head"), None, None),
            P(("seq", "head"), None, None),
            P("seq", None),
        ),
        out_specs=P(("seq", "head"), None, None),
        check_vma=False,
    )
```

```python
import math

import jax
import jax.numpy as jnp
from jax import lax
from jax.experimental import pallas as pl
from jax.experimental.pallas import tpu as pltpu
from jax.sharding import PartitionSpec as P

BLOCK = 128
LEVELS = 6
XS, ZS, CS, YS = 4, 8, 2, 4
PEERS = ZS * CS * YS
PAIRS = ZS * CS
PIECE = 64
NEG = -1e30
MESH = pl.DeviceIdType.MESH


RELAY = 3
AHEAD = PEERS // RELAY + 1
BACK = PEERS - AHEAD
WINDOW = 32
LAG = 8


def kernel(kb_ref, k_ref, v_ref, q_ref, out_ref, raw, src_ref, kv, stage, qs, bias, own_bias, outs, scores, *sems):
    in_sem, kv_send, kv_recv, q_send, q_recv, b_send, b_recv = sems[:7]
    up_send, upa_recv, upb_recv, down_send, down_recv, on_send, two_recv, o_send, o_recv = sems[7:]
    loads = [pltpu.make_async_copy(ref, raw.at[n], in_sem.at[n]) for n, ref in enumerate((k_ref, v_ref, q_ref))]
    for load in loads:
        load.start()
    seq = lax.axis_index("seq")
    y = lax.axis_index("head")
    x = seq // (ZS * CS)
    pair = seq % PAIRS
    z = pair // CS
    core = pair % CS
    my_head = y * PAIRS + pair
    my_slot = pair * YS + y

    def device_of(x_, pair_, y_):
        return (x_ * PAIRS + pair_, y_)

    def offset(i):
        j = i // (CS * YS)
        return ((j + 1) // 2) * (2 * (j % 2) - 1) + ZS, (i // YS) % CS, i % YS

    def toward(i):
        dz, dc, dy = offset(i)
        return ((z + dz) % ZS) * CS + (core + dc) % CS, (y + dy) % YS

    def behind(i):
        dz, dc, dy = offset(i)
        return ((z + 2 * ZS - dz) % ZS) * CS + (core + CS - dc) % CS, (y + YS - dy) % YS

    barrier = pltpu.get_barrier_semaphore()

    def greet(i, carry):
        pair_, y_ = toward(i)
        pl.semaphore_signal(barrier, inc=1, device_id=device_of(x, pair_, y_), device_id_type=MESH)
        return carry

    lax.fori_loop(1, PEERS, greet, 0)
    x_up, x_down = (x + 1) % XS, (x + XS - 1) % XS
    for x_ in (x_up, x_down):
        pl.semaphore_signal(barrier, inc=1, device_id=device_of(x_, pair, y), device_id_type=MESH)

    for block in range(2):
        for level in range(LEVELS):
            for key in range(2):
                key_id = 2 * (seq - 2**level) + key
                hit = (kb_ref[block, 0] == key_id)
                for entry in range(1, 2 * LEVELS):
                    hit = hit | (kb_ref[block, entry] == key_id)
                hit = hit | (key_id == 2 * seq + block - 1)
                value = jnp.where(hit & (key_id >= 0), jnp.float32(0.0), jnp.float32(NEG))
                own_bias[block * 8 + level : block * 8 + level + 1, key * BLOCK : (key + 1) * BLOCK] = jnp.full(
                    (1, BLOCK), value, jnp.float32
                )

    @pl.when(x == 0)
    def _():
        kv[PEERS : 2 * PEERS] = jnp.zeros((PEERS, 2 * PIECE, 128), kv.dtype)

    @pl.when(x <= 1)
    def _():
        kv[0:PEERS] = jnp.zeros((PEERS, 2 * PIECE, 128), kv.dtype)

    near = 2 * PEERS

    def by_head(part):
        loads[part].wait()
        for group in range(0, PEERS, 16):
            src_ref[group : group + 16, part * PIECE : (part + 1) * PIECE, :] = pltpu.einshape(
                "thd->htd", raw[part, :, group : group + 16, :]
            )

    by_head(0)
    by_head(1)
    own_kv = pltpu.make_async_copy(src_ref.at[my_head, pl.ds(0, 2 * PIECE)], kv.at[near + my_slot], kv_recv.at[0])
    own_kv.start()
    pl.semaphore_wait(barrier, PEERS - 1 + 2)

    def send_kv(i, carry):
        pair_, y_ = toward(i)
        pltpu.make_async_remote_copy(
            src_ref.at[y_ * PAIRS + pair_, pl.ds(0, 2 * PIECE)],
            kv.at[near + my_slot],
            kv_send.at[0],
            kv_recv.at[i],
            device_id=device_of(x, pair_, y_),
            device_id_type=MESH,
        ).start()
        return carry

    def send_q(i, carry):
        pair_, y_ = toward(PEERS - i)
        pltpu.make_async_remote_copy(
            src_ref.at[y_ * PAIRS + pair_, pl.ds(2 * PIECE, PIECE)],
            qs.at[my_slot],
            q_send.at[0],
            q_recv.at[pair],
            device_id=device_of(x, pair_, y_),
            device_id_type=MESH,
        ).start()
        return carry

    def send_bias(i, carry):
        pair_, y_ = toward(YS * i)
        pltpu.make_async_remote_copy(
            own_bias, bias.at[pair], b_send.at[0], b_recv.at[0], device_id=device_of(x, pair_, y_), device_id_type=MESH
        ).start()
        return carry

    lax.fori_loop(1, WINDOW, send_kv, 0)
    by_head(2)
    own_q = pltpu.make_async_copy(src_ref.at[my_head, pl.ds(2 * PIECE, PIECE)], qs.at[my_slot], q_recv.at[pair])
    own_q.start()
    own_b = pltpu.make_async_copy(own_bias, bias.at[pair], b_recv.at[0])
    own_b.start()
    lax.fori_loop(1, PAIRS, send_bias, 0)

    def arrived(piece, recv):
        pltpu.make_async_copy(piece, piece, recv).wait()

    def piece_of(i):
        pair_, y_ = behind(i)
        return pair_ * YS + y_

    def pass_on(source, target, send, recv, x_):
        pltpu.make_async_remote_copy(
            source, target, send, recv, device_id=device_of(x_, pair, y), device_id_type=MESH
        ).start()

    def forward(i):
        slot = piece_of(i)
        here = kv.at[near + slot]
        arrived(here, kv_recv.at[i])
        ahead = i % RELAY == 0

        @pl.when((x < XS - 1) & ahead)
        def _():
            pass_on(here, kv.at[near - PEERS + slot], up_send.at[0], upa_recv.at[i // RELAY], x_up)

        @pl.when((x < XS - 1) & jnp.logical_not(ahead))
        def _():
            pass_on(here, kv.at[near - PEERS + slot], up_send.at[0], upb_recv.at[0], x_up)

        @pl.when((x < 2) & jnp.logical_not(ahead))
        def _():
            pass_on(here, stage.at[slot], down_send.at[0], down_recv.at[i], x_down)

    def relay(i):
        slot = piece_of(i)
        ahead = i % RELAY == 0

        @pl.when((x >= 1) & ahead)
        def _():
            here = kv.at[near - PEERS + slot]
            arrived(here, upa_recv.at[i // RELAY])

            @pl.when(x < XS - 1)
            def _():
                pass_on(here, kv.at[slot], on_send.at[0], two_recv.at[0], x_up)

        @pl.when(((x == 0) | (x == XS - 1)) & jnp.logical_not(ahead))
        def _():
            here = stage.at[slot]
            arrived(here, down_recv.at[i])
            pass_on(here, kv.at[slot], on_send.at[0], two_recv.at[0], x_down)

    def both_steps(i, carry):
        forward(i)

        @pl.when(i + WINDOW < PEERS)
        def _():
            send_kv(i + WINDOW, 0)

        @pl.when(i + WINDOW >= PEERS)
        def _():
            first = 1 + 2 * (i + WINDOW - PEERS)
            lax.fori_loop(first, jnp.minimum(first + 2, PEERS), send_q, 0)

        @pl.when(i >= LAG)
        def _():
            relay(i - LAG)

        return carry

    lax.fori_loop(0, PEERS, both_steps, 0)

    def last_steps(i, carry):
        relay(i)
        return carry

    lax.fori_loop(PEERS - LAG, PEERS, last_steps, 0)

    @pl.when(x >= 1)
    def _():
        arrived(kv.at[pl.ds(near - PEERS, BACK)], upb_recv.at[0])

    @pl.when(x >= 2)
    def _():
        arrived(kv.at[pl.ds(0, PEERS)], two_recv.at[0])

    arrived(bias, b_recv.at[0])

    scale = math.log2(math.e) / math.sqrt(128.0)

    def half(p, d, part):
        return kv[pl.ds(YS * (2 * PAIRS + p - d), YS), part * PIECE : (part + 1) * PIECE, :].reshape(2 * BLOCK, 128)

    def attend(p):
        q = qs[pl.ds(YS * p, YS)].reshape(2 * BLOCK, 128)
        peak = None
        for level in range(LEVELS + 1):
            d = 0 if level == LEVELS else 2**level
            s = lax.dot_general(q, half(p, d, 0), (((1,), (1,)), ((), ())), preferred_element_type=jnp.float32)
            if d == 0:
                row = lax.broadcasted_iota(jnp.int32, (2 * BLOCK, 2 * BLOCK), 0)
                col = lax.broadcasted_iota(jnp.int32, (2 * BLOCK, 2 * BLOCK), 1)
                s = jnp.where(col <= row, s, NEG)
                scores[level] = s
            else:
                s0 = s[0:BLOCK] + bias[p, level : level + 1, :]
                s1 = s[BLOCK:] + bias[p, 8 + level : 9 + level, :]
                s = jnp.concatenate([s0, s1], axis=0)
                scores[level] = s
            top = jnp.maximum(s[:, 0:BLOCK], s[:, BLOCK:])
            peak = top if peak is None else jnp.maximum(peak, top)
        peak = jnp.max(peak, axis=1, keepdims=True)
        total = None
        acc = None
        for level in range(LEVELS + 1):
            d = 0 if level == LEVELS else 2**level
            w = jnp.exp2((scores[level] - peak) * scale)
            part = w[:, 0:BLOCK] + w[:, BLOCK:]
            total = part if total is None else total + part
            o = jnp.dot(w.astype(jnp.bfloat16), half(p, d, 1), preferred_element_type=jnp.float32)
            acc = o if acc is None else acc + o
        norm = jnp.sum(total, axis=1, keepdims=True)
        outs[pl.ds(YS * p, YS)] = (acc / norm).astype(jnp.bfloat16).reshape(YS, PIECE, 128)

    def give_back(p):
        for y_ in range(YS):
            here = outs.at[YS * p + y_]
            there = out_ref.at[my_head]
            mine = (p == pair) & (y == y_)

            @pl.when(mine)
            def _():
                pltpu.make_async_copy(here, there, o_recv.at[0]).start()

            @pl.when(jnp.logical_not(mine))
            def _():
                pltpu.make_async_remote_copy(
                    here, there, o_send.at[0], o_recv.at[0], device_id=device_of(x, p, y_), device_id_type=MESH
                ).start()

    def turn(k):
        return toward(YS * (PAIRS - 1 - k))[0]

    def step(k, carry):
        p = turn(k)
        arrived(qs.at[pl.ds(YS * p, YS)], q_recv.at[p])
        attend(p)

        @pl.when(k >= 1)
        def _():
            give_back(turn(k - 1))

        return carry

    lax.fori_loop(0, PAIRS, step, 0)
    give_back(turn(PAIRS - 1))

    arrived(kv.at[pl.ds(near, PEERS - 1)], kv_send.at[0])
    arrived(qs.at[pl.ds(0, PEERS - 1)], q_send.at[0])
    arrived(bias.at[pl.ds(0, PAIRS - 1)], b_send.at[0])

    @pl.when(x < XS - 1)
    def _():
        arrived(kv.at[pl.ds(near, PEERS)], up_send.at[0])

    @pl.when(x < 2)
    def _():
        arrived(stage.at[pl.ds(0, BACK)], down_send.at[0])

    @pl.when((x >= 1) & (x < XS - 1))
    def _():
        arrived(kv.at[pl.ds(0, AHEAD)], on_send.at[0])

    @pl.when((x == 0) | (x == XS - 1))
    def _():
        arrived(kv.at[pl.ds(0, BACK)], on_send.at[0])

    arrived(outs.at[pl.ds(0, PEERS - 1)], o_send.at[0])
    arrived(out_ref, o_recv.at[0])


def local(queries, key_vectors, value_vectors, key_blocks):
    dma = pltpu.SemaphoreType.DMA
    result = pl.pallas_call(
        kernel,
        out_shape=jax.ShapeDtypeStruct((PEERS, PIECE, 128), jnp.bfloat16),
        in_specs=[pl.BlockSpec(memory_space=pltpu.SMEM)] + [pl.BlockSpec(memory_space=pltpu.HBM)] * 3,
        out_specs=pl.BlockSpec(memory_space=pltpu.VMEM),
        scratch_shapes=[
            pltpu.VMEM((3, PIECE, PEERS, 128), jnp.bfloat16),
            pltpu.VMEM((PEERS, 3 * PIECE, 128), jnp.bfloat16),
            pltpu.VMEM((3 * PEERS, 2 * PIECE, 128), jnp.bfloat16),
            pltpu.VMEM((PEERS, 2 * PIECE, 128), jnp.bfloat16),
            pltpu.VMEM((PEERS, PIECE, 128), jnp.bfloat16),
            pltpu.VMEM((PAIRS, 16, 2 * BLOCK), jnp.float32),
            pltpu.VMEM((16, 2 * BLOCK), jnp.float32),
            pltpu.VMEM((PEERS, PIECE, 128), jnp.bfloat16),
            pltpu.VMEM((LEVELS + 1, 2 * BLOCK, 2 * BLOCK), jnp.float32),
            dma((3,)),
            dma((1,)), dma((PEERS,)),
            dma((1,)), dma((PAIRS,)),
            dma((1,)), dma((1,)),
            dma((1,)), dma((AHEAD,)), dma((1,)),
            dma((1,)), dma((PEERS,)),
            dma((1,)), dma((1,)),
            dma((1,)), dma((1,)),
        ],
        compiler_params=pltpu.CompilerParams(collective_id=0, has_side_effects=True, vmem_limit_bytes=48 * 2**20),
    )(key_blocks, key_vectors, value_vectors, queries)
    return jnp.transpose(result, (1, 0, 2))


def solution(mesh):
    return jax.shard_map(
        local,
        mesh=mesh,
        in_specs=(
            P(("seq", "head"), None, None),
            P(("seq", "head"), None, None),
            P(("seq", "head"), None, None),
            P("seq", None),
        ),
        out_specs=P(("seq", "head"), None, None),
        check_vma=False,
    )
```
